256 devices in a mesh: seq: 16 (over y, z_hi), fsdp: 16 (over x, z_lo, core).
Axes of the slice: x: 4, y: 4, z: 8 (z_hi: 4, z_lo: 2; z = z_hi * 2 + z_lo), core: 2. Of those that a mesh axis runs over, the one named last changes fastest.
Arguments:
- tokens: bfloat16 [2048, 4096], P('seq', 'fsdp'), may hold values from -6 to 6
- in_weight: bfloat16 [3, 4096, 4096], P(None, 'seq', 'fsdp'), may hold values from -0.09375 to 0.09375
- out_weight: bfloat16 [4096, 4096], P('fsdp', 'seq'), may hold values from -0.09375 to 0.09375
- filters: float32 [4096, 128], P('fsdp'), may hold values from -0.5 to 0.5
- cotangent: bfloat16 [2048, 4096], P('seq', 'fsdp'), may hold values from -6 to 6
Outputs:
- mixed_out: bfloat16 [2048, 4096], P('seq', 'fsdp')
- grad_tokens: bfloat16 [2048, 4096], P('seq', 'fsdp')
- grad_in_weight: float32 [3, 4096, 4096], P(None, 'seq', 'fsdp')
- grad_out_weight: float32 [4096, 4096], P('fsdp', 'seq')
- grad_filters: float32 [4096, 128], P('fsdp')
The draws below stay inside these ranges and needn't reach their ends.
All inputs are finite; a program needn't handle non-finite values.
Results may differ from the reference program's by a relative error of at most 0.018.
Values may be sent and summed in bfloat16 or wider, within the bound.
A program may use at most 64 MiB of HBM per device.

```python
import jax
import jax.numpy as jnp
from jax import lax

D = 4096
C = 4096
TAPS = 128
TOK_DEV = 128
TOKENS = 2048
N_SEQ = 16
N_FSDP = 16


def raised(array, key, source, target, shards_of, factor):
    def block_of(axis_at):
        return (jnp.arange(array.shape[axis_at]) // (array.shape[axis_at] // shards_of)).reshape((-1,) + (1,) * (array.ndim - 1 - axis_at))

    one_side = jax.random.permutation(key, shards_of)[block_of(target)]
    other_side = (block_of(target) + shards_of // 2) % shards_of
    return jnp.where((block_of(source) == one_side) | (block_of(source) == other_side), factor * array, array)


def block_levels(rng, shape, shards, low, top_value):
    factor_of, own = 1.0, jax.random.fold_in(rng, 6)
    for dim, parts in shards:
        draws = jnp.exp(jax.random.uniform(jax.random.fold_in(own, dim), (parts,), jnp.float32, low / len(shards), top_value / len(shards)))
        factor_of = factor_of * jnp.repeat(draws, shape[dim] // parts).reshape([-1 if axis == dim else 1 for axis in range(len(shape))])
    return factor_of


def scatter_about(rng, shape, deviation, limit, pieces=(), held_as=jnp.bfloat16):
    entries = jax.random.normal(rng, shape, jnp.float32) * deviation
    if len(pieces) > 0:
        entries = block_levels(rng, shape, pieces, -0.22, 0.18) * entries
    return jnp.clip(entries, min=-limit, max=limit).astype(held_as)


def bell_draw_with(rng, extent, scale, limit, cuts, heavy, kind=jnp.bfloat16):
    array = scale * jax.random.normal(rng, extent, jnp.float32)
    if cuts:
        array = array * block_levels(rng, extent, cuts, -0.22, 0.18)
    return jnp.clip(raised(array, jax.random.fold_in(rng, 3), *heavy), -limit, limit).astype(kind)


def setup_inputs(seed: int = 0) -> dict:
    key_of = jax.random.split(jax.random.key(seed), 6)
    tokens = bell_draw_with(key_of[0], (TOKENS, D), 1.0, 6.0, ((0, 16), (1, 16)), (0, 1, 16, 2.0))
    in_weight = scatter_about(key_of[1], (3, D, C), D ** -0.5, 0.09375, ((1, 16), (2, 16)))
    out_weight = scatter_about(key_of[2], (C, D), C ** -0.5, 0.09375, ((0, 16), (1, 16)))
    filters = scatter_about(key_of[3], (C, TAPS), TAPS ** -0.5, 0.5, ((0, 16),), jnp.float32)
    cotangent = bell_draw_with(key_of[4], (TOKENS, D), 1.0, 6.0, ((0, 16), (1, 16)), (0, 1, 16, 2.0))
    return {"tokens": tokens, "in_weight": in_weight, "out_weight": out_weight, "filters": filters, "cotangent": cotangent}


def causal_filter(extended, filters):
    length = extended.shape[0] - filters.shape[1] + 1
    margin = filters.shape[1] - 1
    weights = jnp.transpose(filters)

    def add_tap(index, running):
        start = (margin - index).astype(jnp.int32)
        piece = lax.dynamic_slice_in_dim(extended, start, length, 0)
        tap_row = lax.dynamic_slice_in_dim(weights, index.astype(jnp.int32), 1, 0)
        return running + piece * tap_row
    start_sum = jnp.zeros((length, filters.shape[0]), jnp.float32)
    return lax.fori_loop(jnp.int32(0), jnp.int32(filters.shape[1]), add_tap, start_sum)

def reverse_filter(extended, filters):
    length = extended.shape[0] - filters.shape[1] + 1
    weights = jnp.transpose(filters)

    def add_tap(index, running):
        piece = lax.dynamic_slice_in_dim(extended, index.astype(jnp.int32), length, 0)
        tap_row = lax.dynamic_slice_in_dim(weights, index.astype(jnp.int32), 1, 0)
        return running + piece * tap_row
    start_sum = jnp.zeros((length, filters.shape[0]), jnp.float32)
    return lax.fori_loop(jnp.int32(0), jnp.int32(filters.shape[1]), add_tap, start_sum)

def filter_grad(extended, gradient, taps):
    length = gradient.shape[0]
    margin = taps - 1

    def one_tap(index):
        start = (margin - index).astype(jnp.int32)
        piece = lax.dynamic_slice_in_dim(extended, start, length, 0)
        return lax.optimization_barrier(jnp.sum(piece * gradient, axis=0))
    columns = lax.map(one_tap, jnp.arange(taps, dtype=jnp.int32))
    return jnp.transpose(columns)

def rounded(value):
    return lax.optimization_barrier(value.astype(jnp.bfloat16)).astype(jnp.float32)

def reference(tokens, in_weight, out_weight, filters, cotangent):
    margin = TAPS - 1
    channels = C // N_FSDP
    projected = jnp.einsum('td,idc->itc', tokens.astype(jnp.float32), in_weight.astype(jnp.float32)).astype(jnp.bfloat16)
    queries = projected[0].astype(jnp.float32)
    key_part = projected[1].astype(jnp.float32)
    value_part = projected[2].astype(jnp.float32)
    signal = (key_part * value_part).astype(jnp.bfloat16)
    zero_rows = jnp.zeros((margin, C), jnp.float32)
    extended = jnp.concatenate([zero_rows, signal.astype(jnp.float32)], 0)
    filtered = causal_filter(extended, filters)
    gated_rows = (queries * filtered).astype(jnp.bfloat16)
    gated_blocks = jnp.transpose(gated_rows.reshape(TOKENS, N_FSDP, channels), (1, 0, 2))
    out_blocks = out_weight.reshape(N_FSDP, channels, D)

    def add_mixed(running, pair):
        return (running + rounded(jnp.dot(pair[0], pair[1], preferred_element_type=jnp.float32)), None)
    mixed_sum, unused = lax.scan(add_mixed, jnp.zeros((TOKENS, D), jnp.float32), (gated_blocks, out_blocks))
    mixed_out = mixed_sum.astype(jnp.bfloat16)
    grad_gated = jnp.dot(cotangent, jnp.transpose(out_weight), preferred_element_type=jnp.float32)
    grad_queries = grad_gated * filtered
    grad_filtered = (grad_gated * queries).astype(jnp.bfloat16)
    grad_signal = reverse_filter(jnp.concatenate([grad_filtered.astype(jnp.float32), zero_rows], 0), filters)
    grad_filters = filter_grad(extended, grad_filtered.astype(jnp.float32), TAPS)
    grad_projected = jnp.stack([grad_queries, grad_signal * value_part, grad_signal * key_part]).astype(jnp.bfloat16)
    grad_blocks = jnp.transpose(grad_projected.reshape(3, TOKENS, N_FSDP, channels), (2, 0, 1, 3))
    weight_blocks = jnp.transpose(in_weight.reshape(3, D, N_FSDP, channels), (2, 0, 1, 3))

    def add_input(running, pair):
        term = jnp.einsum('itc,idc->td', pair[0].astype(jnp.float32), pair[1].astype(jnp.float32))
        return (running + rounded(term), None)
    grad_sum, unused = lax.scan(add_input, jnp.zeros((TOKENS, D), jnp.float32), (grad_blocks, weight_blocks))
    grad_tokens = grad_sum.astype(jnp.bfloat16)
    token_blocks = tokens.reshape(N_SEQ, TOK_DEV, D)
    proj_blocks = jnp.transpose(grad_projected.reshape(3, N_SEQ, TOK_DEV, C), (1, 0, 2, 3))
    gate_blocks = gated_rows.reshape(N_SEQ, TOK_DEV, C)
    cot_blocks = cotangent.reshape(N_SEQ, TOK_DEV, D)

    def add_weights(running, group):
        term_in = jnp.einsum('td,itc->idc', group[0].astype(jnp.float32), group[1].astype(jnp.float32))
        term_out = jnp.dot(jnp.transpose(group[2]), group[3], preferred_element_type=jnp.float32)
        return ((running[0] + rounded(term_in), running[1] + rounded(term_out)), None)
    start_sums = (jnp.zeros((3, D, C), jnp.float32), jnp.zeros((C, D), jnp.float32))
    weight_sums, unused = lax.scan(add_weights, start_sums, (token_blocks, proj_blocks, gate_blocks, cot_blocks))
    return (mixed_out, grad_tokens, weight_sums[0], weight_sums[1], grad_filters)
```

```python
import functools

import jax
import jax.numpy as jnp
from jax import lax
from jax.experimental import pallas as pl
from jax.experimental.pallas import tpu as pltpu

highest = lax.Precision.HIGHEST
MESH = pl.DeviceIdType.MESH
f32 = jnp.float32
bf16 = jnp.bfloat16


class Place:
    def __init__(self):
        self.s = lax.axis_index("seq")
        self.f = lax.axis_index("fsdp")
        self.y, self.zh = self.s // 4, self.s % 4
        self.x, self.w = self.f // 4, self.f % 4
        self.zl, self.core = self.w // 2, self.w % 2

    def y_at(self, step):
        return (self.y + 4 + step) % 4

    def z_at(self, step):
        return (self.zh + 4 + step) % 4

    def x_at(self, step):
        return (self.x + 4 + step) % 4

    def y_dev(self, step):
        return (self.y_at(step) * 4 + self.zh, self.f)

    def z_dev(self, step):
        return (self.y * 4 + self.z_at(step), self.f)

    def x_dev(self, step):
        return (self.s, self.x_at(step) * 4 + self.w)

    def other_core(self):
        return (self.s, self.f + 1 - 2 * self.core)

    def s_dev(self, step):
        return ((self.s + 16 + step) % 16, self.f)

    def spread(self, zl):
        return (self.y * 4 + self.w, self.x * 4 + zl * 2 + self.zh % 2)

    def origin(self, half):
        return (self.y * 4 + half * 2 + self.core, self.x * 4 + self.zh)

    def is_me(self, dev):
        return jnp.logical_and(dev[0] == self.s, dev[1] == self.f)


def pos(a):
    return (a % 2) * 2 + a // 2


class Net:
    def __init__(self, place, send, recv):
        self.place, self.send, self.recv = place, send, recv
        self.n_send = self.n_recv = 0
        self.ends = []

    def slots(self, count):
        first = self.n_recv
        self.n_recv += count
        return first

    def copy(self, src, dst, dev, slot=None, may_be_me=False):
        if slot is None:
            slot = self.slots(1)
        out = self.send.at[self.n_send]
        self.n_send += 1
        far = pltpu.make_async_remote_copy(
            src_ref=src, dst_ref=dst, send_sem=out, recv_sem=self.recv.at[slot],
            device_id=dev, device_id_type=MESH,
        )
        if may_be_me:
            me = self.place.is_me(dev)
            near = pltpu.make_async_copy(src, dst, self.recv.at[slot])
            pl.when(me)(near.start)
            pl.when(jnp.logical_not(me))(far.start)
            self.ends.append(lambda: pl.when(jnp.logical_not(me))(far.wait_send))
        else:
            far.start()
            self.ends.append(far.wait_send)
        return far

    def arrived(self, ref, slot):
        pltpu.make_async_copy(ref, ref, self.recv.at[slot]).wait()

    def finish(self):
        for end in self.ends:
            end()


def meet(others):
    barrier = pltpu.get_barrier_semaphore()
    for dev in others:
        pl.semaphore_signal(barrier, inc=1, device_id=dev, device_id_type=MESH)
    pl.semaphore_wait(barrier, len(others))


class RingGather:
    def __init__(self, net, dev, at, block, half, own):
        self.net, self.dev, self.at, self.block, self.half = net, dev, at, block, half
        here = block(at(0))
        self.up = net.copy(own, here, dev(1))
        self.down = net.copy(own, here, dev(-1))

    def relay(self):
        self.up.wait_recv()
        self.far_up = self.net.copy(
            self.half(self.at(-1), 0), self.half(self.at(-1), 0), self.dev(1))
        self.down.wait_recv()
        self.far_down = self.net.copy(
            self.half(self.at(1), 1), self.half(self.at(1), 1), self.dev(-1))

    def wait(self):
        self.far_up.wait_recv()
        self.far_down.wait_recv()


class RingReduce:
    def __init__(self, net, dev, at, out, far_in, near_in, cut):
        self.net, self.dev, self.at = net, dev, at
        self.out, self.far_in, self.near_in, self.cut = out, far_in, near_in, cut

    def start_far(self, value):
        self.out[0] = value.astype(bf16)
        a, b = self.cut
        self.f_up = self.net.copy(self.out.at[(0,) + a], self.far_in.at[0], self.dev(1))
        self.f_down = self.net.copy(self.out.at[(0,) + b], self.far_in.at[1], self.dev(-1))

    def start_near(self, up, down):
        self.read_up, self.read_down = up, down
        a, b = self.cut
        self.out[(1,) + b] = up(b).astype(bf16)
        self.n_up = self.net.copy(self.out.at[(1,) + b], self.near_in.at[(0,) + b], self.dev(1))
        self.out[(2,) + a] = down(a).astype(bf16)
        self.n_down = self.net.copy(self.out.at[(2,) + a], self.near_in.at[(1,) + a], self.dev(-1))

    def relay(self):
        a, b = self.cut
        self.f_up.wait_recv()
        self.out[(1,) + a] = (self.read_up(a) + self.far_in[0].astype(f32)).astype(bf16)
        self.r_up = self.net.copy(self.out.at[(1,) + a], self.near_in.at[(0,) + a], self.dev(1))
        self.f_down.wait_recv()
        self.out[(2,) + b] = (self.read_down(b) + self.far_in[1].astype(f32)).astype(bf16)
        self.r_down = self.net.copy(self.out.at[(2,) + b], self.near_in.at[(1,) + b], self.dev(-1))

    def result(self, own):
        for copy in (self.n_up, self.n_down, self.r_up, self.r_down):
            copy.wait_recv()
        return own + self.near_in[0].astype(f32) + self.near_in[1].astype(f32)


class Activations:
    def __init__(self, net, place, own, full):
        self.net, self.place, self.full = net, place, full
        self.first = net.slots(2)
        self.core_copies = []
        for zl in range(2):
            net.copy(own, full.at[place.x, pos(place.zh)], place.spread(zl),
                     slot=self.first + place.zh // 2, may_be_me=True)

    def unit(self, b, lo=0, n=2):
        return self.full.at[b, pl.ds(self.place.core * 2 + lo, n)]

    def to_core(self, ref):
        self.core_copies.append(self.net.copy(ref, ref, self.place.other_core()))

    def ring(self):
        place = self.place
        for half in range(2):
            self.net.arrived(self.full.at[place.x, place.core * 2 + half], self.first + half)
        self.gather = RingGather(
            self.net, place.x_dev, place.x_at, self.unit,
            lambda b, h: self.unit(b, h, 1), self.unit(place.x))
        self.to_core(self.unit(place.x))

    def relay(self):
        self.gather.relay()
        self.to_core(self.unit(self.place.x_at(-1)))
        self.to_core(self.unit(self.place.x_at(1)))

    def far(self):
        self.gather.wait()
        self.to_core(self.unit(self.place.x_at(2)))

    def wait(self):
        for copy in self.core_copies:
            copy.wait_recv()


def dot(a, b, ca, cb):
    return lax.dot_general(a, b, (((ca,), (cb,)), ((), ())), preferred_element_type=f32)


def rows512(value):
    return value.reshape(512, 256)


def forward_kernel(tok, cot, win, wout,
                   kvq_o, gg_o, sig_o, gf_o, xg_o, cg_o, wg_o, wo_o,
                   xg, cg, wg, wo, part, z_out, z_far, z_near, halo, mine, send, recv, local):
    place = Place()
    near = [place.y_dev(1), place.y_dev(-1), place.z_dev(1), place.z_dev(-1), place.x_dev(1),
            place.x_dev(-1), place.other_core(), place.s_dev(1), place.s_dev(-1)]
    far = [place.spread(0), place.spread(1), place.origin(0), place.origin(1)]
    meet(near + far)
    net = Net(place, send, recv)

    xs = Activations(net, place, tok, xg)
    half_rows = (pl.ds(0, 128), pl.ds(128, 128))

    def weight(own, full):
        return RingGather(net, place.y_dev, place.y_at, lambda b: full.at[b],
                          lambda b, h: full.at[b, half_rows[h]], own)

    wk = weight(win.at[1], wg.at[1])
    cs = Activations(net, place, cot, cg)
    wv = weight(win.at[2], wg.at[2])
    wu = weight(wout, wo)
    wq = weight(win.at[0], wg.at[0])
    for i in range(3):
        wg[i, place.y] = win[i]
    wo[place.y] = wout[...]

    xs.ring()
    cs.ring()
    wk.relay()
    xs.relay()
    wv.relay()
    cs.relay()
    wu.relay()
    wq.relay()
    xs.far()
    cs.far()

    cut = ((pl.ds(0, 64),), (pl.ds(64, 64),))

    def reduce(slot, left, right, transposed):
        total = None
        for b in range(4):
            term = dot(rows512(left[b]), right(b), 1, 1 if transposed else 0)
            total = term if total is None else total + term
        part[slot] = total.reshape(4, 128, 256)
        ring = RingReduce(net, place.z_dev, place.z_at, z_out.at[slot], z_far.at[slot],
                          z_near.at[slot], cut)
        ring.start_far(part[slot, pos(place.z_at(2))])
        ring.start_near(lambda rows: part[(slot, pos(place.z_at(1))) + rows],
                        lambda rows: part[(slot, pos(place.z_at(-1))) + rows])
        return ring

    stores = []

    def keep(src, dst):
        copy = pltpu.make_async_copy(src, dst, local.at[len(stores)])
        copy.start()
        stores.append(copy)

    xs.wait()
    keep(xg, xg_o)
    wk.wait()
    rk = reduce(0, xg, lambda b: wg[1, b], False)
    wv.wait()
    rv = reduce(1, xg, lambda b: wg[2, b], False)
    rk.relay()
    cs.wait()
    keep(cg, cg_o)
    wu.wait()
    keep(wo, wo_o)
    ru = reduce(2, cg, lambda b: wo[b], True)
    rv.relay()
    wq.wait()
    keep(wg, wg_o)
    rq = reduce(3, xg, lambda b: wg[0, b], False)
    me = pos(place.zh)
    k = rk.result(part[0, me]).astype(bf16)
    ru.relay()
    v = rv.result(part[1, me]).astype(bf16)
    kvq_o[0] = k
    kvq_o[1] = v
    mine[0] = (k.astype(f32) * v.astype(f32)).astype(bf16)
    after = net.copy(mine.at[0], halo.at[0], place.s_dev(1))
    rq.relay()
    gg = ru.result(part[2, me])
    gg_o[...] = gg
    q = rq.result(part[3, me]).astype(bf16)
    kvq_o[2] = q
    mine[1] = (gg * q.astype(f32)).astype(bf16)
    before = net.copy(mine.at[1], halo.at[1], place.s_dev(-1))
    sig_o[1] = mine[0]
    gf_o[0] = mine[1]
    after.wait_recv()
    sig_o[0] = jnp.where(place.s == 0, jnp.zeros((128, 256), bf16), halo[0])
    before.wait_recv()
    gf_o[1] = jnp.where(place.s == 15, jnp.zeros((128, 256), bf16), halo[1])
    for copy in stores:
        copy.wait()
    net.finish()


def backward_kernel(gated, gp, gfilt, xg_i, cg_i, wg_i, wo_i,
                    mixed_o, gtok_o, gin_o, gout_o, gfilt_o,
                    xg, cg, wg, wo, ag, keep_g, y_out, y_far, y_near,
                    part, c_out, c_in, x_out, x_far, x_near, fin_out, fin_in,
                    fz_out, fz_far, fz_near, fy, fz, send, recv, local):
    place = Place()
    near = [place.y_dev(1), place.y_dev(-1), place.z_dev(1), place.z_dev(-1), place.x_dev(1),
            place.x_dev(-1), place.other_core()]
    far = [place.spread(0), place.spread(1), place.origin(0), place.origin(1)]
    loads = []
    for src, dst in ((wo_i, wo), (cg_i, cg), (xg_i, xg), (wg_i, wg)):
        copy = pltpu.make_async_copy(src, dst, local.at[len(loads)])
        copy.start()
        loads.append(copy)
    meet(near + far)
    net = Net(place, send, recv)

    half_rows = (pl.ds(0, 64), pl.ds(64, 64))

    def acts(own, i):
        full = ag.at[i]
        return RingGather(net, place.z_dev, place.z_at, lambda a: full.at[pos(a)],
                          lambda a, h: full.at[pos(a), half_rows[h]], own)

    gathers = [acts(gated, 0)] + [acts(gp.at[i], i + 1) for i in range(3)]
    ag[0, pos(place.zh)] = gated[...]
    for i in range(3):
        ag[i + 1, pos(place.zh)] = gp[i]

    y_cut = ((pl.ds(0, 128),), (pl.ds(128, 128),))

    def weight_grad(slot, block):
        ring = RingReduce(net, place.y_dev, place.y_at, y_out.at[slot], y_far.at[slot],
                          y_near.at[slot], y_cut)
        ring.start_far(block(place.y_at(2)))
        keep_g[slot, 0] = block(place.y_at(1))
        keep_g[slot, 1] = block(place.y_at(-1))
        ring.start_near(lambda rows: keep_g[(slot, 0) + rows], lambda rows: keep_g[(slot, 1) + rows])
        keep_g[slot, 2] = block(place.y_at(0))
        return ring

    x_cut = ((pl.ds(0, 1),), (pl.ds(1, 1),))

    class Features:
        def __init__(self, slot, block):
            self.slot, self.swaps = slot, []
            for j, step in enumerate((2, 1, -1, 0)):
                part[slot, j] = block(place.x_at(step)).reshape(4, 128, 256)
                c_out[slot, j] = part[slot, j, pl.ds((1 - place.core) * 2, 2)].astype(bf16)
                self.swaps.append(net.copy(c_out.at[slot, j], c_in.at[slot, j], place.other_core()))

        def both(self, j, rows=None):
            base = place.core * 2
            if rows is None:
                return part[self.slot, j, pl.ds(base, 2)] + c_in[self.slot, j].astype(f32)
            lo = rows[0].start
            return (part[self.slot, j, pl.ds(base + lo, 1)]
                    + c_in[self.slot, j, pl.ds(lo, 1)].astype(f32))

        def ring(self):
            slot = self.slot
            self.reduce = RingReduce(net, place.x_dev, place.x_at, x_out.at[slot], x_far.at[slot],
                                     x_near.at[slot], x_cut)
            self.swaps[0].wait_recv()
            self.reduce.start_far(self.both(0))
            self.swaps[1].wait_recv()
            self.swaps[2].wait_recv()
            self.reduce.start_near(lambda rows: self.both(1, rows), lambda rows: self.both(2, rows))

        def relay(self):
            self.reduce.relay()

        def last(self):
            slot = self.slot
            self.swaps[3].wait_recv()
            fin_out[slot] = self.reduce.result(self.both(3)).astype(bf16)
            self.first = net.slots(2)
            for half in range(2):
                net.copy(fin_out.at[slot, half], fin_in.at[slot, place.zl], place.origin(half),
                         slot=self.first + place.zl, may_be_me=True)

        def result(self):
            for zl in range(2):
                net.arrived(fin_in.at[self.slot, zl], self.first + zl)
            return (fin_in[self.slot, 0].astype(f32) + fin_in[self.slot, 1].astype(f32)).astype(bf16)

    f_cut = ((pl.ds(0, 32),), (pl.ds(32, 32),))
    fr = RingReduce(net, place.z_dev, place.z_at, fz_out, fz_far, fz_near, f_cut)
    fr.start_far(gfilt[place.z_at(2)])
    fr.start_near(lambda rows: gfilt[(place.z_at(1),) + rows],
                  lambda rows: gfilt[(place.z_at(-1),) + rows])

    gathers[0].relay()
    gathers[1].relay()
    gathers[0].wait()
    loads[0].wait()
    loads[1].wait()
    mixed = Features(0, lambda b: dot(rows512(ag[0]), wo[b], 1, 0))
    grads = [weight_grad(0, lambda b: dot(rows512(ag[0]), rows512(cg[b]), 0, 0))]
    gathers[2].relay()
    fr.relay()
    gathers[1].wait()
    loads[2].wait()

    def in_grad(i):
        return weight_grad(i + 1, lambda b: dot(rows512(xg[b]), rows512(ag[i + 1]), 0, 0))

    grads.append(in_grad(0))
    mixed.ring()
    gathers[3].relay()
    gathers[2].wait()
    grads.append(in_grad(1))
    grads[0].relay()
    mixed.relay()
    fy[place.y] = fr.result(gfilt[place.zh]).astype(bf16)
    fyg = RingGather(net, place.y_dev, place.y_at, lambda b: fy.at[b],
                     lambda b, h: fy.at[b, (pl.ds(0, 32), pl.ds(32, 32))[h]], fy.at[place.y])
    gathers[3].wait()
    loads[3].wait()

    def token_block(b):
        total = dot(rows512(ag[1]), wg[0, b], 1, 1)
        for i in (1, 2):
            total = total + dot(rows512(ag[i + 1]), wg[i, b], 1, 1)
        return total

    gtok = Features(1, token_block)
    grads.append(in_grad(2))
    grads[1].relay()
    mixed.last()
    gtok.ring()
    fyg.relay()
    grads[2].relay()
    gtok.relay()
    grads[3].relay()
    gout_o[...] = grads[0].result(keep_g[0, 2])
    gin_o[0] = grads[1].result(keep_g[1, 2])
    fyg.wait()
    fz[place.zh] = (fy[0].astype(f32) + fy[1].astype(f32) + fy[2].astype(f32)
                    + fy[3].astype(f32)).astype(bf16)
    fzg = RingGather(net, place.z_dev, place.z_at, lambda b: fz.at[b],
                     lambda b, h: fz.at[b, (pl.ds(0, 32), pl.ds(32, 32))[h]], fz.at[place.zh])
    gtok.last()
    fzg.relay()
    mixed_o[...] = mixed.result()
    gin_o[1] = grads[2].result(keep_g[2, 2])
    gin_o[2] = grads[3].result(keep_g[3, 2])
    fzg.wait()
    gfilt_o[...] = fz[...].astype(f32)
    gtok_o[...] = gtok.result()
    net.finish()


def vmem(*shape, kind=bf16):
    return pltpu.VMEM(shape, kind)


def shape_of(*shape, kind=bf16):
    return jax.ShapeDtypeStruct(shape, kind)


def in_vmem():
    return pl.BlockSpec(memory_space=pltpu.VMEM)


def in_place():
    return pl.BlockSpec(memory_space=pl.ANY)


def forward(tokens, cotangent, in_weight, out_weight):
    return pl.pallas_call(
        forward_kernel,
        out_shape=(
            shape_of(3, 128, 256), shape_of(128, 256, kind=f32), shape_of(2, 128, 256),
            shape_of(2, 128, 256), shape_of(4, 4, 128, 256), shape_of(4, 4, 128, 256),
            shape_of(3, 4, 256, 256), shape_of(4, 256, 256)),
        in_specs=[in_vmem()] * 4,
        out_specs=(in_vmem(),) * 4 + (in_place(),) * 4,
        scratch_shapes=[
            vmem(4, 4, 128, 256), vmem(4, 4, 128, 256), vmem(3, 4, 256, 256), vmem(4, 256, 256),
            vmem(4, 4, 128, 256, kind=f32), vmem(4, 3, 128, 256), vmem(4, 2, 64, 256),
            vmem(4, 2, 128, 256), vmem(2, 128, 256), vmem(2, 128, 256),
            pltpu.SemaphoreType.DMA((80,)), pltpu.SemaphoreType.DMA((80,)),
            pltpu.SemaphoreType.DMA((4,))],
        compiler_params=pltpu.CompilerParams(
            collective_id=0, has_side_effects=True, vmem_limit_bytes=56 * 2 ** 20),
        name="forward_exchange",
    )(tokens, cotangent, in_weight, out_weight)


def backward(gated, gp, gfilt, xg, cg, wg, wo):
    return pl.pallas_call(
        backward_kernel,
        out_shape=(
            shape_of(128, 256), shape_of(128, 256), shape_of(3, 256, 256, kind=f32),
            shape_of(256, 256, kind=f32), shape_of(4, 64, 128, kind=f32)),
        in_specs=[in_vmem()] * 3 + [in_place()] * 4,
        out_specs=(in_vmem(),) * 5,
        scratch_shapes=[
            vmem(4, 4, 128, 256), vmem(4, 4, 128, 256), vmem(3, 4, 256, 256), vmem(4, 256, 256),
            vmem(4, 4, 128, 256), vmem(4, 3, 256, 256, kind=f32), vmem(4, 3, 256, 256),
            vmem(4, 2, 128, 256), vmem(4, 2, 256, 256),
            vmem(2, 4, 4, 128, 256, kind=f32), vmem(2, 4, 2, 128, 256), vmem(2, 4, 2, 128, 256),
            vmem(2, 3, 2, 128, 256), vmem(2, 2, 1, 128, 256), vmem(2, 2, 2, 128, 256),
            vmem(2, 2, 128, 256), vmem(2, 2, 128, 256),
            vmem(3, 64, 128), vmem(2, 32, 128), vmem(2, 64, 128), vmem(4, 64, 128),
            vmem(4, 64, 128),
            pltpu.SemaphoreType.DMA((96,)), pltpu.SemaphoreType.DMA((96,)),
            pltpu.SemaphoreType.DMA((4,))],
        compiler_params=pltpu.CompilerParams(
            collective_id=1, has_side_effects=True, vmem_limit_bytes=56 * 2 ** 20),
        name="backward_exchange",
    )(gated, gp, gfilt, xg, cg, wg, wo)


def causal_filter(extended, filters):
    kernel = jnp.flip(jnp.transpose(filters), 0)[:, None, :]
    result = lax.conv_general_dilated(
        extended[None], kernel, (1,), "VALID", dimension_numbers=("NWC", "WIO", "NWC"),
        feature_group_count=filters.shape[0], precision=highest)
    return result[0]


def reverse_filter(extended, filters):
    kernel = jnp.transpose(filters)[:, None, :]
    result = lax.conv_general_dilated(
        extended[None], kernel, (1,), "VALID", dimension_numbers=("NWC", "WIO", "NWC"),
        feature_group_count=filters.shape[0], precision=highest)
    return result[0]


def filter_grad(extended, gradient):
    result = lax.conv_general_dilated(
        extended[None], gradient[:, None, :], (1,), "VALID",
        dimension_numbers=("NWC", "WIO", "NWC"), feature_group_count=gradient.shape[1],
        precision=highest)
    return jnp.transpose(jnp.flip(result[0], 0))


def on_device(tokens, in_weight, out_weight, filters, cotangent):
    kvq, grad_gated, signal, grads, xg, cg, wg, wo = forward(
        tokens, cotangent, in_weight, out_weight)
    key_part, value_part, queries = (kvq[i].astype(f32) for i in range(3))
    extended = signal.reshape(256, 256).astype(f32)[1:]
    later = grads.reshape(256, 256).astype(f32)[:-1]
    filtered = causal_filter(extended, filters)
    gated = (queries * filtered).astype(bf16)
    grad_signal = reverse_filter(later, filters)
    grad_filters = filter_grad(extended, grads[0].astype(f32))
    grad_projected = jnp.stack(
        [grad_gated * filtered, grad_signal * value_part, grad_signal * key_part]).astype(bf16)
    mixed, grad_tokens, grad_in, grad_out, grad_filters = backward(
        gated, grad_projected, grad_filters.reshape(4, 64, 128), xg, cg, wg, wo)
    return mixed, grad_tokens, grad_in, grad_out, grad_filters.reshape(256, 128)


def solution(mesh):
    placed = (
        jax.P("seq", "fsdp"),
        jax.P(None, "seq", "fsdp"),
        jax.P("fsdp", "seq"),
        jax.P("fsdp", None),
        jax.P("seq", "fsdp"),
    )
    return jax.shard_map(
        on_device,
        mesh=mesh,
        in_specs=placed,
        out_specs=(
            jax.P("seq", "fsdp"),
            jax.P("seq", "fsdp"),
            jax.P(None, "seq", "fsdp"),
            jax.P("fsdp", "seq"),
            jax.P("fsdp", None),
        ),
        check_vma=False,
    )
```

```python
import functools

import jax
import jax.numpy as jnp
from jax import lax
from jax.experimental import pallas as pl
from jax.experimental.pallas import tpu as pltpu

MESH = pl.DeviceIdType.MESH
f32 = jnp.float32
bf16 = jnp.bfloat16


class Place:
    def __init__(self):
        self.s = lax.axis_index("seq")
        self.f = lax.axis_index("fsdp")
        self.y, self.zh = self.s // 4, self.s % 4
        self.x, self.w = self.f // 4, self.f % 4
        self.zl, self.core = self.w // 2, self.w % 2

    def y_at(self, step):
        return (self.y + 4 + step) % 4

    def z_at(self, step):
        return (self.zh + 4 + step) % 4

    def x_at(self, step):
        return (self.x + 4 + step) % 4

    def y_dev(self, step):
        return (self.y_at(step) * 4 + self.zh, self.f)

    def z_dev(self, step):
        return (self.y * 4 + self.z_at(step), self.f)

    def x_dev(self, step):
        return (self.s, self.x_at(step) * 4 + self.w)

    def other_core(self):
        return (self.s, self.f + 1 - 2 * self.core)

    def s_dev(self, step):
        return ((self.s + 16 + step) % 16, self.f)

    def spread(self, zl):
        return (self.y * 4 + self.w, self.x * 4 + zl * 2 + self.zh % 2)

    def origin(self, half):
        return (self.y * 4 + half * 2 + self.core, self.x * 4 + self.zh)

    def is_me(self, dev):
        return jnp.logical_and(dev[0] == self.s, dev[1] == self.f)


def pos(a):
    return (a % 2) * 2 + a // 2


class Net:
    def __init__(self, place, send, recv):
        self.place, self.send, self.recv = place, send, recv
        self.n_send = self.n_recv = 0
        self.ends = []

    def slots(self, count):
        first = self.n_recv
        self.n_recv += count
        return first

    def copy(self, src, dst, dev, slot=None, may_be_me=False):
        if slot is None:
            slot = self.slots(1)
        out = self.send.at[self.n_send]
        self.n_send += 1
        far = pltpu.make_async_remote_copy(
            src_ref=src, dst_ref=dst, send_sem=out, recv_sem=self.recv.at[slot],
            device_id=dev, device_id_type=MESH,
        )
        if may_be_me:
            me = self.place.is_me(dev)
            near = pltpu.make_async_copy(src, dst, self.recv.at[slot])
            pl.when(me)(near.start)
            pl.when(jnp.logical_not(me))(far.start)
            self.ends.append(lambda: pl.when(jnp.logical_not(me))(far.wait_send))
        else:
            far.start()
            self.ends.append(far.wait_send)
        return far

    def arrived(self, ref, slot):
        pltpu.make_async_copy(ref, ref, self.recv.at[slot]).wait()

    def finish(self):
        for end in self.ends:
            end()


def meet(others):
    barrier = pltpu.get_barrier_semaphore()
    for dev in others:
        pl.semaphore_signal(barrier, inc=1, device_id=dev, device_id_type=MESH)
    pl.semaphore_wait(barrier, len(others))


class RingGather:
    def __init__(self, net, dev, at, block, half, own):
        self.net, self.dev, self.at, self.block, self.half = net, dev, at, block, half
        here = block(at(0))
        self.up = net.copy(own, here, dev(1))
        self.down = net.copy(own, here, dev(-1))

    def relay(self):
        self.up.wait_recv()
        self.far_up = self.net.copy(
            self.half(self.at(-1), 0), self.half(self.at(-1), 0), self.dev(1))
        self.down.wait_recv()
        self.far_down = self.net.copy(
            self.half(self.at(1), 1), self.half(self.at(1), 1), self.dev(-1))

    def wait(self):
        self.far_up.wait_recv()
        self.far_down.wait_recv()


class RingReduce:
    def __init__(self, net, dev, at, out, far_in, near_in, cut):
        self.net, self.dev, self.at = net, dev, at
        self.out, self.far_in, self.near_in, self.cut = out, far_in, near_in, cut

    def start_far(self, value):
        self.out[0] = value.astype(bf16)
        a, b = self.cut
        self.f_up = self.net.copy(self.out.at[(0,) + a], self.far_in.at[0], self.dev(1))
        self.f_down = self.net.copy(self.out.at[(0,) + b], self.far_in.at[1], self.dev(-1))

    def start_near(self, up, down):
        self.read_up, self.read_down = up, down
        a, b = self.cut
        self.out[(1,) + b] = up(b).astype(bf16)
        self.n_up = self.net.copy(self.out.at[(1,) + b], self.near_in.at[(0,) + b], self.dev(1))
        self.out[(2,) + a] = down(a).astype(bf16)
        self.n_down = self.net.copy(self.out.at[(2,) + a], self.near_in.at[(1,) + a], self.dev(-1))

    def relay(self):
        a, b = self.cut
        self.f_up.wait_recv()
        self.out[(1,) + a] = (self.read_up(a) + self.far_in[0].astype(f32)).astype(bf16)
        self.r_up = self.net.copy(self.out.at[(1,) + a], self.near_in.at[(0,) + a], self.dev(1))
        self.f_down.wait_recv()
        self.out[(2,) + b] = (self.read_down(b) + self.far_in[1].astype(f32)).astype(bf16)
        self.r_down = self.net.copy(self.out.at[(2,) + b], self.near_in.at[(1,) + b], self.dev(-1))

    def result(self, own):
        for copy in (self.n_up, self.n_down, self.r_up, self.r_down):
            copy.wait_recv()
        return own + self.near_in[0].astype(f32) + self.near_in[1].astype(f32)


class Activations:
    def __init__(self, net, place, own, full):
        self.net, self.place, self.full = net, place, full
        self.first = net.slots(2)
        self.core_copies = []
        for zl in range(2):
            net.copy(own, full.at[place.x, pos(place.zh)], place.spread(zl),
                     slot=self.first + place.zh // 2, may_be_me=True)

    def unit(self, b, lo=0, n=2):
        return self.full.at[b, pl.ds(self.place.core * 2 + lo, n)]

    def to_core(self, ref):
        self.core_copies.append(self.net.copy(ref, ref, self.place.other_core()))

    def ring(self):
        place = self.place
        for half in range(2):
            self.net.arrived(self.full.at[place.x, place.core * 2 + half], self.first + half)
        self.gather = RingGather(
            self.net, place.x_dev, place.x_at, self.unit,
            lambda b, h: self.unit(b, h, 1), self.unit(place.x))
        self.to_core(self.unit(place.x))

    def relay(self):
        self.gather.relay()
        self.to_core(self.unit(self.place.x_at(-1)))
        self.to_core(self.unit(self.place.x_at(1)))

    def far(self):
        self.gather.wait()
        self.to_core(self.unit(self.place.x_at(2)))

    def wait(self):
        for copy in self.core_copies:
            copy.wait_recv()


def dot(a, b, ca=1, cb=0):
    return lax.dot_general(a, b, (((ca,), (cb,)), ((), ())), preferred_element_type=f32)


def rows512(value):
    return value.reshape(512, 256)


def side_by_side(values):
    return jnp.concatenate(values, axis=1)


def filter_sum(taps, shifted, start):
    halves = []
    for h in range(2):
        def step(jj, total):
            eight = taps[h, jj]
            first = pl.multiple_of(start(jj), 8)
            for r in range(8):
                total = total + eight[r:r + 1] * shifted[r, h, pl.ds(first, 128)]
            return total
        halves.append(lax.fori_loop(0, 16, step, jnp.zeros((128, 128), f32)))
    return side_by_side(halves)


def block_kernel(tok, cot, win, wout, filters,
                 mixed_o, gtok_o, gin_o, gout_o, gfilt_o,
                 xg, cg, wg, wo, xt, part, z_out, z_far, z_near, halo, mine, kvq,
                 taps, ext, shifted, tap_grads, gfilt,
                 ag, keep_g, y_out, y_far, y_near, feat, c_out, c_in, x_out, x_far, x_near,
                 fin_out, fin_in, fz_out, fz_far, fz_near, fy, fz,
                 mixed_v, gtok_v, grads_v, gfilt_v, send, recv, local):
    place = Place()
    others = [place.y_dev(1), place.y_dev(-1), place.z_dev(1), place.z_dev(-1), place.x_dev(1),
              place.x_dev(-1), place.other_core(), place.s_dev(1), place.s_dev(-1),
              place.spread(0), place.spread(1), place.origin(0), place.origin(1)]
    meet(others)
    net = Net(place, send, recv)
    half_rows = (pl.ds(0, 128), pl.ds(128, 128))

    def weight(own, full):
        return RingGather(net, place.y_dev, place.y_at, lambda b: full.at[b],
                          lambda b, h: full.at[b, half_rows[h]], own)

    xs = Activations(net, place, tok, xg)
    wk = weight(win.at[1], wg.at[1])
    cs = Activations(net, place, cot, cg)
    wv = weight(win.at[2], wg.at[2])
    for i in range(3):
        wg[i, place.y] = win[i]
    wo[place.y] = wout[...]
    turned = jnp.transpose(filters[...])
    for h in range(2):
        taps[h] = turned[:, h * 128:(h + 1) * 128].reshape(16, 8, 128)

    cut = ((pl.ds(0, 64),), (pl.ds(64, 64),))

    def reduce(slot, left, right, transposed):
        total = dot(side_by_side([rows512(left[b]) for b in range(4)]), right,
                    1, 1 if transposed else 0)
        part[slot] = total.reshape(4, 128, 256)
        ring = RingReduce(net, place.z_dev, place.z_at, z_out.at[slot], z_far.at[slot],
                          z_near.at[slot], cut)
        ring.start_far(part[slot, pos(place.z_at(2))])
        ring.start_near(lambda rows: part[(slot, pos(place.z_at(1))) + rows],
                        lambda rows: part[(slot, pos(place.z_at(-1))) + rows])
        return ring

    def turn(b):
        xt[b] = jnp.transpose(rows512(xg[b]))

    xs.ring()
    wk.relay()
    wq = weight(win.at[0], wg.at[0])
    cs.ring()
    xs.relay()
    wv.relay()
    wu = weight(wout, wo)
    xs.far()
    wk.wait()
    xs.wait()
    rk = reduce(0, xg, wg[1].reshape(1024, 256), False)
    wq.relay()
    wv.wait()
    rv = reduce(1, xg, wg[2].reshape(1024, 256), False)
    cs.relay()
    rk.relay()
    wu.relay()
    cs.far()
    wq.wait()
    rq = reduce(2, xg, wg[0].reshape(1024, 256), False)
    rv.relay()
    cs.wait()
    wu.wait()
    ru = reduce(3, cg, side_by_side([wo[b] for b in range(4)]), True)
    me = pos(place.zh)
    k = rk.result(part[0, me]).astype(bf16)
    kvq[0] = k
    rq.relay()
    v = rv.result(part[1, me]).astype(bf16)
    kvq[1] = v
    signal = (k.astype(f32) * v.astype(f32)).astype(bf16)
    mine[0] = signal
    after = net.copy(mine.at[0], halo.at[0], place.s_dev(1))

    def extend(lo, value):
        value = value.astype(f32)
        for h in range(2):
            ext[h, lo:lo + 128] = value[:, h * 128:(h + 1) * 128]

    extend(128, signal)
    turn(0)
    ru.relay()
    turn(1)
    after.wait_recv()
    extend(0, jnp.where(place.s == 0, jnp.zeros((128, 256), bf16), halo[0]))
    for r in range(8):
        for h in range(2):
            shifted[r, h, 8:256] = ext[h, 8 - r:256 - r]
    filtered = filter_sum(taps, shifted, lambda jj: 128 - 8 * jj)
    q = rq.result(part[2, me]).astype(bf16)

    quarter = (pl.ds(0, 64), pl.ds(64, 64))

    def acts(i, value):
        full = ag.at[i]
        full[me] = value.astype(bf16)
        return RingGather(net, place.z_dev, place.z_at, lambda a: full.at[pos(a)],
                          lambda a, h: full.at[pos(a), quarter[h]], full.at[me])

    gathers = [acts(0, q.astype(f32) * filtered)]
    gg = ru.result(part[3, me])
    grad_filtered = (gg * q.astype(f32)).astype(bf16)
    mine[1] = grad_filtered
    before = net.copy(mine.at[1], halo.at[1], place.s_dev(-1))
    gathers.append(acts(1, gg * filtered))

    gradient = grad_filtered.astype(f32)
    for h in range(2):
        side = gradient[:, h * 128:(h + 1) * 128]

        def one(jj, unused):
            first = pl.multiple_of(128 - 8 * jj, 8)
            tap_grads[h, jj] = jnp.concatenate(
                [jnp.sum(side * shifted[r, h, pl.ds(first, 128)], axis=0, keepdims=True)
                 for r in range(8)], axis=0)
            return unused
        lax.fori_loop(0, 16, one, 0)
    gathers[0].relay()
    extend(0, mine[1])
    before.wait_recv()
    extend(128, jnp.where(place.s == 15, jnp.zeros((128, 256), bf16), halo[1]))
    for r in range(8):
        for h in range(2):
            shifted[r, h, 0:248] = ext[h, r:248 + r]
    grad_signal = filter_sum(taps, shifted, lambda jj: 8 * jj)
    gathers.append(acts(2, grad_signal * kvq[1].astype(f32)))
    gathers[1].relay()
    gathers.append(acts(3, grad_signal * kvq[0].astype(f32)))

    f_cut = ((pl.ds(0, 32),), (pl.ds(32, 32),))
    for h in range(2):
        turned = jnp.transpose(tap_grads[h].reshape(128, 128))
        gfilt[2 * h] = turned[0:64]
        gfilt[2 * h + 1] = turned[64:128]
    fr = RingReduce(net, place.z_dev, place.z_at, fz_out, fz_far, fz_near, f_cut)
    fr.start_far(gfilt[place.z_at(2)])
    fr.start_near(lambda rows: gfilt[(place.z_at(1),) + rows],
                  lambda rows: gfilt[(place.z_at(-1),) + rows])

    y_cut = ((pl.ds(0, 128),), (pl.ds(128, 128),))

    def weight_grad(slot, block):
        ring = RingReduce(net, place.y_dev, place.y_at, y_out.at[slot], y_far.at[slot],
                          y_near.at[slot], y_cut)
        ring.start_far(block(place.y_at(2)))
        keep_g[slot, 0] = block(place.y_at(1))
        keep_g[slot, 1] = block(place.y_at(-1))
        ring.start_near(lambda rows: keep_g[(slot, 0) + rows], lambda rows: keep_g[(slot, 1) + rows])
        keep_g[slot, 2] = block(place.y_at(0))
        return ring

    x_cut = ((pl.ds(0, 1),), (pl.ds(1, 1),))

    class Features:
        def __init__(self, slot, block):
            self.slot, self.swaps = slot, []
            for j, step in enumerate((2, 1, -1, 0)):
                feat[slot, j] = block(place.x_at(step)).reshape(4, 128, 256)
                c_out[slot, j] = feat[slot, j, pl.ds((1 - place.core) * 2, 2)].astype(bf16)
                self.swaps.append(net.copy(c_out.at[slot, j], c_in.at[slot, j], place.other_core()))

        def both(self, j, rows=(pl.ds(0, 2),)):
            lo, n = rows[0].start, rows[0].size
            return (feat[self.slot, j, pl.ds(place.core * 2 + lo, n)]
                    + c_in[self.slot, j, pl.ds(lo, n)].astype(f32))

        def ring(self):
            slot = self.slot
            self.reduce = RingReduce(net, place.x_dev, place.x_at, x_out.at[slot], x_far.at[slot],
                                     x_near.at[slot], x_cut)
            self.swaps[0].wait_recv()
            self.reduce.start_far(self.both(0))
            self.swaps[1].wait_recv()
            self.swaps[2].wait_recv()
            self.reduce.start_near(lambda rows: self.both(1, rows), lambda rows: self.both(2, rows))

        def relay(self):
            self.reduce.relay()

        def last(self):
            slot = self.slot
            self.swaps[3].wait_recv()
            fin_out[slot] = self.reduce.result(self.both(3)).astype(bf16)
            self.first = net.slots(2)
            for half in range(2):
                net.copy(fin_out.at[slot, half], fin_in.at[slot, place.zl], place.origin(half),
                         slot=self.first + place.zl, may_be_me=True)

        def result(self):
            for zl in range(2):
                net.arrived(fin_in.at[self.slot, zl], self.first + zl)
            return (fin_in[self.slot, 0].astype(f32) + fin_in[self.slot, 1].astype(f32)).astype(bf16)

    stores = []

    def put(value, stage, out):
        stage[...] = value
        copy = pltpu.make_async_copy(stage, out, local.at[len(stores)])
        copy.start()
        stores.append(copy)

    gathers[0].wait()
    mixed = Features(0, lambda b: dot(rows512(ag[0]), wo[b]))
    gathers[2].relay()
    turned_gated = jnp.transpose(rows512(ag[0]))
    grads = [weight_grad(0, lambda b: dot(turned_gated, rows512(cg[b])))]
    gathers[3].relay()
    turn(2)
    turn(3)
    fr.relay()
    gathers[1].wait()

    def in_grad(i):
        return weight_grad(i + 1, lambda b: dot(xt[b], rows512(ag[i + 1])))

    mixed.ring()
    grads.append(in_grad(0))
    grads[0].relay()
    gathers[2].wait()
    grads.append(in_grad(1))
    mixed.relay()
    fy[place.y] = fr.result(gfilt[place.zh]).astype(bf16)
    f_half = (pl.ds(0, 32), pl.ds(32, 32))
    fyg = RingGather(net, place.y_dev, place.y_at, lambda b: fy.at[b],
                     lambda b, h: fy.at[b, f_half[h]], fy.at[place.y])
    grads[1].relay()
    gathers[3].wait()
    left = side_by_side([rows512(ag[i + 1]) for i in range(3)])
    gtok = Features(1, lambda b: dot(left, side_by_side([wg[i, b] for i in range(3)]), 1, 1))
    gtok.ring()
    grads.append(in_grad(2))
    gtok.relay()
    mixed.last()
    grads[2].relay()
    fyg.relay()
    gtok.last()
    grads[3].relay()
    put(grads[0].result(keep_g[0, 2]), grads_v.at[3], gout_o)
    put(grads[1].result(keep_g[1, 2]), grads_v.at[0], gin_o.at[0])
    fyg.wait()
    fz[place.zh] = (fy[0].astype(f32) + fy[1].astype(f32) + fy[2].astype(f32)
                    + fy[3].astype(f32)).astype(bf16)
    fzg = RingGather(net, place.z_dev, place.z_at, lambda b: fz.at[b],
                     lambda b, h: fz.at[b, f_half[h]], fz.at[place.zh])
    put(mixed.result(), mixed_v, mixed_o)
    put(grads[2].result(keep_g[2, 2]), grads_v.at[1], gin_o.at[1])
    fzg.relay()
    put(grads[3].result(keep_g[3, 2]), grads_v.at[2], gin_o.at[2])
    put(gtok.result(), gtok_v, gtok_o)
    fzg.wait()
    put(fz[...].astype(f32), gfilt_v, gfilt_o)
    for copy in stores:
        copy.wait()
    net.finish()


def hand_on_kernel(*refs):
    sources, outs, stages, loads, stores = refs[:5], refs[5:10], refs[10:15], refs[15], refs[16]
    coming = [pltpu.make_async_copy(s, v, loads.at[i]) for i, (s, v) in enumerate(zip(sources, stages))]
    for copy in coming:
        copy.start()
    going = [pltpu.make_async_copy(v, o, stores.at[i]) for i, (v, o) in enumerate(zip(stages, outs))]
    for first, second in zip(coming, going):
        first.wait()
        second.start()
    for copy in going:
        copy.wait()


def vmem(*shape, kind=bf16):
    return pltpu.VMEM(shape, kind)


def shape_of(*shape, kind=bf16):
    return jax.ShapeDtypeStruct(shape, kind)


def in_vmem():
    return pl.BlockSpec(memory_space=pltpu.VMEM)


def in_place():
    return pl.BlockSpec(memory_space=pl.ANY)


results = (
    shape_of(128, 256), shape_of(128, 256), shape_of(3, 256, 256, kind=f32),
    shape_of(256, 256, kind=f32), shape_of(4, 64, 128, kind=f32))


def on_device(tokens, in_weight, out_weight, filters, cotangent):
    exchanged = pl.pallas_call(
        block_kernel,
        out_shape=results,
        in_specs=[in_vmem()] * 5,
        out_specs=(in_place(),) * 5,
        scratch_shapes=[
            vmem(4, 4, 128, 256), vmem(4, 4, 128, 256), vmem(3, 4, 256, 256), vmem(4, 256, 256),
            vmem(4, 256, 512),
            vmem(4, 4, 128, 256, kind=f32), vmem(4, 3, 128, 256), vmem(4, 2, 64, 256),
            vmem(4, 2, 128, 256), vmem(2, 128, 256), vmem(2, 128, 256), vmem(2, 128, 256),
            vmem(2, 16, 8, 128, kind=f32), vmem(2, 256, 128, kind=f32),
            vmem(8, 2, 256, 128, kind=f32), vmem(2, 16, 8, 128, kind=f32),
            vmem(4, 64, 128, kind=f32),
            vmem(4, 4, 128, 256), vmem(4, 3, 256, 256, kind=f32), vmem(4, 3, 256, 256),
            vmem(4, 2, 128, 256), vmem(4, 2, 256, 256),
            vmem(2, 4, 4, 128, 256, kind=f32), vmem(2, 4, 2, 128, 256), vmem(2, 4, 2, 128, 256),
            vmem(2, 3, 2, 128, 256), vmem(2, 2, 1, 128, 256), vmem(2, 2, 2, 128, 256),
            vmem(2, 2, 128, 256), vmem(2, 2, 128, 256),
            vmem(3, 64, 128), vmem(2, 32, 128), vmem(2, 64, 128), vmem(4, 64, 128),
            vmem(4, 64, 128),
            vmem(128, 256), vmem(128, 256), vmem(4, 256, 256, kind=f32),
            vmem(4, 64, 128, kind=f32),
            pltpu.SemaphoreType.DMA((176,)), pltpu.SemaphoreType.DMA((176,)),
            pltpu.SemaphoreType.DMA((8,))],
        compiler_params=pltpu.CompilerParams(
            collective_id=0, has_side_effects=True, vmem_limit_bytes=60 * 2 ** 20),
        name="block_exchange",
    )(tokens, cotangent, in_weight, out_weight, filters)
    mixed, grad_tokens, grad_in, grad_out, grad_filters = pl.pallas_call(
        hand_on_kernel,
        out_shape=results,
        in_specs=[in_place()] * 5,
        out_specs=(in_place(),) * 5,
        scratch_shapes=[pltpu.VMEM(r.shape, r.dtype) for r in results]
        + [pltpu.SemaphoreType.DMA((5,)), pltpu.SemaphoreType.DMA((5,))],
        name="hand_on",
    )(*exchanged)
    return mixed, grad_tokens, grad_in, grad_out, grad_filters.reshape(256, 128)


def solution(mesh):
    placed = (
        jax.P("seq", "fsdp"),
        jax.P(None, "seq", "fsdp"),
        jax.P("fsdp", "seq"),
        jax.P("fsdp", None),
        jax.P("seq", "fsdp"),
    )
    return jax.shard_map(
        on_device,
        mesh=mesh,
        in_specs=placed,
        out_specs=(
            jax.P("seq", "fsdp"),
            jax.P("seq", "fsdp"),
            jax.P(None, "seq", "fsdp"),
            jax.P("fsdp", "seq"),
            jax.P("fsdp", None),
        ),
        check_vma=False,
    )
```
